32 devices in a mesh: dp: 8 (over y, x, core), tensor: 4 (over z).
Axes of the slice: x: 2, y: 2, z: 4, core: 2. Of those that a mesh axis runs over, the one named last changes fastest.
Arguments:
- tokens: bfloat16 [18432, 1024], P(('dp', 'tensor')), may hold values from -6 to 6
- cotangent: bfloat16 [18432, 1024], P(('dp', 'tensor')), may hold values from -6 to 6
- deal: int32 [18432], P(('dp', 'tensor')), may hold values from 0 to 18431, as said below
- source: int32 [18432], P(('dp', 'tensor')), may hold values from 0 to 18431, as said below
- lengths: int32 [8, 2, 3], P('dp'), may hold values from 1 to 1024, 1152 in all within a row
- qkv_weight: bfloat16 [3, 1024, 1024], P(None, 'dp', 'tensor'), may hold values from -0.1875 to 0.1875
- query_bias: bfloat16 [1024], replicated, may hold values from -3 to 3
- value_bias: bfloat16 [1024], replicated, may hold values from -3 to 3
- out_weight: bfloat16 [1024, 1024], P('tensor', 'dp'), may hold values from -3 to 3
- out_bias: bfloat16 [1024], replicated, may hold values from -3 to 3
- first_gain: bfloat16 [1024], replicated, may hold values from 0.5 to 1.5
- first_shift: bfloat16 [1024], replicated, may hold values from -3 to 3
- up_weight: bfloat16 [1024, 4096], P('dp', 'tensor'), may hold values from -0.1875 to 0.1875
- up_bias: bfloat16 [4096], replicated, may hold values from -3 to 3
- down_weight: bfloat16 [4096, 1024], P('tensor', 'dp'), may hold values from -0.09375 to 0.09375
- down_bias: bfloat16 [1024], replicated, may hold values from -3 to 3
- second_gain: bfloat16 [1024], replicated, may hold values from 0.5 to 1.5
- second_shift: bfloat16 [1024], replicated, may hold values from -3 to 3
Outputs:
- layer_out: bfloat16 [18432, 1024], P(('dp', 'tensor'))
- tokens_grad: float32 [18432, 1024], P(('dp', 'tensor'))
- qkv_grad: float32 [3, 1024, 1024], P(None, 'dp', 'tensor')
- query_bias_grad: float32 [1024], replicated
- value_bias_grad: float32 [1024], replicated
- out_weight_grad: float32 [1024, 1024], P('tensor', 'dp')
- out_bias_grad: float32 [1024], replicated
- first_gain_grad: float32 [1024], replicated
- first_shift_grad: float32 [1024], replicated
- up_weight_grad: float32 [1024, 4096], P('dp', 'tensor')
- up_bias_grad: float32 [4096], replicated
- down_weight_grad: float32 [4096, 1024], P('tensor', 'dp')
- down_bias_grad: float32 [1024], replicated
- second_gain_grad: float32 [1024], replicated
- second_shift_grad: float32 [1024], replicated
The draws below stay inside these ranges and needn't reach their ends.
Inputs may be any that keep to these rules, and one draw needn't show every extreme that they name: A permutation: given row g becomes work row deal[g]. The given rows of an aligned block of 576 with block index c all go to blocks of 576 work rows whose index has the same remainder as c modulo 4, exactly 72 rows into each of them. The inverse of deal: source[deal[g]] = g.
All inputs are finite; a program needn't handle non-finite values.
Results may differ from the reference program's by a relative error of at most 0.014.
The reference program's roundings to bfloat16 on the way count: a program that leaves them out, or rounds other values in their place, can miss the bound.
Values may be sent and summed in bfloat16 or wider, within the bound.
A program may use at most 256 MiB of HBM per device.

```python
import math
import jax
import jax.numpy as jnp
import numpy as np
from jax import lax

D = 1024
H = 16
DH = 64
FF = 4096
MB = 2
TOK_MB = 1152
LONGEST = 1024
SEQS = 3
SPLIT = 4
ROWS = 576
TOKENS = 18432
N_DP = 8


def deal_tables(key):
    base = jax.random.fold_in(key, 11)
    first_key, second_key = jax.random.split(base)
    data_ways = TOKENS // (SPLIT * ROWS)
    per_peer = ROWS // data_ways
    groups = data_ways * SPLIT
    slot_orders = jax.vmap(lambda one_key: jax.random.permutation(one_key, ROWS))(jax.random.split(first_key, groups))
    senders = (slot_orders // per_peer).reshape(data_ways, SPLIT, ROWS).transpose(1, 0, 2).reshape(SPLIT, data_ways * ROWS)
    work_index = jnp.arange(TOKENS, dtype=jnp.int32).reshape(data_ways, SPLIT, ROWS).transpose(1, 0, 2).reshape(SPLIT, data_ways * ROWS)
    sort_order = jnp.argsort(senders, axis=1, stable=True)
    grouped = jnp.take_along_axis(work_index, sort_order, axis=1).reshape(SPLIT, data_ways, ROWS)
    mixing = jax.vmap(lambda one_key: jax.random.permutation(one_key, ROWS))(jax.random.split(second_key, groups))
    mixing = mixing.reshape(SPLIT, data_ways, ROWS)
    dealt = jnp.take_along_axis(grouped, mixing, axis=2).transpose(1, 0, 2).reshape(TOKENS).astype(jnp.int32)
    inverse = jnp.argsort(dealt, stable=True).astype(jnp.int32)
    return (dealt, inverse)


def draw_deal(key, part):
    return deal_tables(key)[0]


def draw_source(key, part):
    return deal_tables(key)[1]


def steps_of(stream_key, extent, cuts, smallest, largest):
    def one(axis_at, blocks):
        steps = jax.random.uniform(jax.random.fold_in(jax.random.fold_in(stream_key, 6), axis_at), (blocks,), jnp.float32, smallest / len(cuts), largest / len(cuts))
        return jnp.repeat(jnp.exp(steps), extent[axis_at] // blocks).reshape((-1,) + (1,) * (len(extent) - axis_at - 1))

    loudness = one(*cuts[0])
    for cut in cuts[1:]:
        loudness = loudness * one(*cut)
    return loudness


def profile(number_of, total, most, skew):
    loads = [(1 << 20) // math.isqrt(rank ** skew) + 1 for rank in range(2, number_of + 1)]
    rest, given = total - most - (number_of - 1), [1] * (number_of - 1)
    while rest > 0:
        free = [i for i in range(number_of - 1) if given[i] < most]
        mass, budget = sum([loads[i] for i in free]), rest
        for i in free:
            extra = min(most - given[i], max(1, budget * loads[i] // mass), rest)
            given[i] = given[i] + extra
            rest = rest - extra
    return np.array([most] + given)


def ragged(stream_key, count, total, bound, slope):
    if count == 2:
        one = jax.random.randint(stream_key, (), max(1, total - bound), min(bound, total - 1) + 1)
        return jnp.stack([one, total - one])
    tallies = jnp.asarray(profile(count, total, bound, slope), jnp.int32)
    twos = (count - 1) // 2
    donor, receiver = tallies[1:1 + 2 * twos:2], tallies[2:2 + 2 * twos:2]
    slack = jnp.minimum(donor - 1, bound - receiver)
    passed = jax.random.randint(jax.random.fold_in(stream_key, 1), (twos,), 0, 1 << 20) % (slack + 1)
    tallies = tallies.at[1:1 + 2 * twos:2].set(donor - passed).at[2:2 + 2 * twos:2].set(receiver + passed)
    return tallies[jax.random.permutation(jax.random.fold_in(stream_key, 2), count)]


def centred(own_key, extent, scale, reach, shards=(), kind=jnp.bfloat16):
    values = scale * jax.random.normal(own_key, extent, jnp.float32)
    if shards:
        values = values * steps_of(own_key, extent, shards, -0.22, 0.18)
    return jnp.clip(values, -reach, reach).astype(kind)


def setup_inputs(seed: int = 0) -> dict:
    key_list = jax.random.split(jax.random.key(seed), 19)
    tokens = centred(key_list[0], (TOKENS, D), 1.0, 6.0, ((0, 32),))
    cotangent = centred(key_list[1], (TOKENS, D), 1.0, 6.0, ((0, 32),))
    deal = draw_deal(jax.random.fold_in(key_list[18], 71), 0)
    source = draw_source(jax.random.fold_in(key_list[18], 71), 0)
    lengths = jax.vmap(lambda own: ragged(own, SEQS, TOK_MB, LONGEST, 2))(jax.random.split(key_list[4], N_DP * MB)).reshape((N_DP, MB, SEQS)).astype(jnp.int32)
    qkv_weight = centred(key_list[5], (3, D, D), D ** -0.5, 0.1875, ((1, 8), (2, 4)))
    query_bias = centred(key_list[6], (D,), 0.5, 3.0)
    value_bias = centred(key_list[7], (D,), 0.5, 3.0)
    out_weight = centred(key_list[8], (D, D), (max(1, D // 256)) ** -0.5, 3.0, ((0, 4), (1, 8)))
    out_bias = centred(key_list[9], (D,), 0.5, 3.0)
    first_gain = jnp.clip(1.0 + 0.1 * jax.random.normal(key_list[10], (D,), jnp.float32), 0.5, 1.5).astype(jnp.bfloat16)
    first_shift = centred(key_list[11], (D,), 0.5, 3.0)
    up_weight = centred(key_list[12], (D, FF), D ** -0.5, 0.1875, ((0, 8), (1, 4)))
    up_bias = centred(key_list[13], (FF,), 0.5, 3.0)
    down_weight = centred(key_list[14], (FF, D), FF ** -0.5, 0.09375, ((0, 4), (1, 8)))
    down_bias = centred(key_list[15], (D,), 0.5, 3.0)
    second_gain = jnp.clip(1.0 + 0.1 * jax.random.normal(key_list[16], (D,), jnp.float32), 0.5, 1.5).astype(jnp.bfloat16)
    second_shift = centred(key_list[17], (D,), 0.5, 3.0)
    return dict(tokens=tokens, cotangent=cotangent, deal=deal, source=source, lengths=lengths, qkv_weight=qkv_weight, query_bias=query_bias, value_bias=value_bias, out_weight=out_weight, out_bias=out_bias, first_gain=first_gain, first_shift=first_shift, up_weight=up_weight, up_bias=up_bias, down_weight=down_weight, down_bias=down_bias, second_gain=second_gain, second_shift=second_shift)


@jax.custom_vjp
def low(v):
    return lax.optimization_barrier(v.astype(jnp.bfloat16)).astype(jnp.float32)

@jax.custom_vjp
def low_back(v):
    return v

def low_keep(v):
    return (low(v), None)

def low_pass(kept, grad):
    return (grad,)

def back_keep(v):
    return (v, None)

def back_low(kept, grad):
    return (low(grad),)
low.defvjp(low_keep, low_pass)
low_back.defvjp(back_keep, back_low)

def matmul(left_side, right_side):
    return jnp.dot(left_side, right_side, precision=lax.Precision.HIGHEST)

def contract(pattern, left_side, right_side):
    return jnp.einsum(pattern, left_side, right_side, precision=lax.Precision.HIGHEST)

def layer_norm(values, gain_vec, shift_vec):
    center = values - lax.optimization_barrier(jnp.mean(values, axis=-1, keepdims=True))
    spread = lax.optimization_barrier(jnp.mean(center * center, axis=-1, keepdims=True))
    return center * lax.rsqrt(spread + 1e-05) * gain_vec + shift_vec

def encoder(params, inputs, allowed):
    qkv_weight, query_bias, value_bias, out_weight, out_bias, first_gain, first_shift, up_weight, up_bias, down_weight, down_bias, second_gain, second_shift = params
    row_count = inputs.shape[0]
    queries = low(low_back(matmul(inputs, qkv_weight[0])) + query_bias).reshape(row_count, H, DH)
    key_rows = low(low_back(matmul(inputs, qkv_weight[1]))).reshape(row_count, H, DH)
    value_rows = low(low_back(matmul(inputs, qkv_weight[2])) + value_bias).reshape(row_count, H, DH)
    scores = low_back(contract('qhd,khd->hqk', queries, key_rows)) * DH ** (-0.5)
    scores = jnp.where(allowed[None], scores, -1e+30)
    attn_probs = low(jax.nn.softmax(scores, axis=-1))
    mixed_heads = low(low_back(contract('hqk,khd->qhd', attn_probs, value_rows))).reshape(row_count, D)
    first_sum = inputs + low_back(matmul(mixed_heads, out_weight)) + out_bias
    normed = layer_norm(first_sum, first_gain, first_shift)
    pre_act = low_back(matmul(low(normed), up_weight)) + up_bias
    hidden = low(jax.nn.gelu(pre_act, approximate=False))
    second_sum = normed + low_back(matmul(hidden, down_weight)) + down_bias
    return layer_norm(second_sum, second_gain, second_shift)

def reference(tokens, cotangent, deal, source, lengths, qkv_weight, query_bias, value_bias, out_weight, out_bias, first_gain, first_shift, up_weight, up_bias, down_weight, down_bias, second_gain, second_shift):
    params = tuple((array.astype(jnp.float32) for array in (qkv_weight, query_bias, value_bias, out_weight, out_bias, first_gain, first_shift, up_weight, up_bias, down_weight, down_bias, second_gain, second_shift)))
    per_split = TOK_MB // SPLIT

    def to_work(given_rows):
        arranged = given_rows.astype(jnp.float32)[source]
        arranged = arranged.reshape(N_DP, SPLIT, MB, per_split, D).transpose(0, 2, 1, 3, 4)
        return arranged.reshape(N_DP * MB, TOK_MB, D)
    inputs_all = to_work(tokens)
    grads_all = to_work(cotangent)
    lengths_all = lengths.reshape(N_DP * MB, SEQS)
    positions = jnp.arange(TOK_MB, dtype=jnp.int32)

    def one_batch(totals, batch_item):
        inputs, grad_rows, seq_lengths = batch_item
        seq_ends = jnp.cumsum(seq_lengths)
        seq_ids = lax.optimization_barrier(jnp.sum((positions[:, None] >= seq_ends[None, :]).astype(jnp.int32), axis=1))
        allowed = seq_ids[:, None] == seq_ids[None, :]
        result, pullback = jax.vjp(lambda weights, rows_in: encoder(weights, rows_in, allowed), params, inputs)
        weight_grads, input_grads = pullback(grad_rows)
        totals = jax.tree.map(jnp.add, totals, weight_grads)
        return (totals, (result.astype(jnp.bfloat16), input_grads))
    empty_grads = jax.tree.map(jnp.zeros_like, params)
    totals, (outputs, input_grads) = lax.scan(one_batch, empty_grads, (inputs_all, grads_all, lengths_all))

    def to_given(arranged):
        arranged = arranged.reshape(N_DP, MB, SPLIT, per_split, D).transpose(0, 2, 1, 3, 4)
        return arranged.reshape(TOKENS, D)[deal]
    grad_qkv, grad_query, grad_value, grad_out, grad_out_bias, grad_first_gain, grad_first_shift, grad_up, grad_up_bias, grad_down, grad_down_bias, grad_second_gain, grad_second_shift = totals
    return (to_given(outputs), to_given(input_grads), grad_qkv, grad_query, grad_value, grad_out, grad_out_bias, grad_first_gain, grad_first_shift, grad_up, grad_up_bias, grad_down, grad_down_bias, grad_second_gain, grad_second_shift)
```

```python
import jax
import jax.numpy as jnp
from jax import lax
from jax.sharding import Mesh, PartitionSpec as P

DH = 64
MB = 2
F32 = jnp.float32
BF16 = jnp.bfloat16
ALL = ("chip", "core", "tensor")


def shift(x, step):
    n = lax.axis_size("tensor")
    return lax.ppermute(x, "tensor", [(i, (i + step) % n) for i in range(n)])


def flip(x, bit):
    n = lax.axis_size("chip")
    return lax.ppermute(x, "chip", [(i, i ^ bit) for i in range(n)])


def swap(x):
    return lax.ppermute(x, "core", [(0, 1), (1, 0)])


def chip_bits():
    n = lax.axis_size("chip")
    return [1 << i for i in range(n.bit_length() - 1)]


def pick(flag, x, y):
    return jnp.where(flag, x, y)


def ordered(core, mine, theirs, axis):
    return pick(
        core == 0,
        jnp.concatenate([mine, theirs], axis),
        jnp.concatenate([theirs, mine], axis),
    )


def relative(x, axis):
    chip = lax.axis_index("chip")
    n = lax.axis_size("chip")
    depth = x.shape[axis] // n
    for bit in chip_bits():
        parts = [lax.slice_in_dim(x, p * depth, (p + 1) * depth, axis=axis) for p in range(n)]
        other = jnp.concatenate([parts[p ^ bit] for p in range(n)], axis)
        x = pick((chip & bit) != 0, other, x)
    return x


def to_piece(shard, core):
    half = shard.shape[-1] // 2
    keep = lax.dynamic_slice_in_dim(shard, core * half, half, axis=1)
    give = lax.dynamic_slice_in_dim(shard, (1 - core) * half, half, axis=1)
    return ordered(core, keep, swap(give), 0)


def from_piece(piece, core):
    depth = piece.shape[0] // 2
    keep = lax.dynamic_slice_in_dim(piece, core * depth, depth, axis=0)
    give = lax.dynamic_slice_in_dim(piece, (1 - core) * depth, depth, axis=0)
    return ordered(core, keep, swap(give), 1)


def gather_line(piece):
    half = piece.shape[0] // 2
    below = shift(piece, 1)
    above = shift(piece, -1)
    far = jnp.concatenate([shift(below[:half], 1), shift(above[half:], -1)], 0)
    return piece, below, above, far


def gather_chips(unit, bits):
    depth = unit.shape[0]
    order = [0]
    for bit in bits:
        unit = jnp.concatenate([unit, flip(unit, bit)], 0)
        order = order + [p ^ bit for p in order]
    if order == sorted(order):
        return unit
    place = {p: i for i, p in enumerate(order)}
    return jnp.concatenate(
        [unit[place[p] * depth : (place[p] + 1) * depth] for p in range(len(order))], 0
    )


def gather_weight(piece):
    own, below, above, far = gather_line(piece)
    bits = chip_bits()
    return (
        gather_chips(jnp.concatenate([own, below], 1), bits),
        gather_chips(jnp.concatenate([above, far], 1), bits[::-1]),
    )


def scatter_chips(grad, bits):
    n = lax.axis_size("chip")
    depth = grad.shape[0] // n
    blocks = [grad[p * depth : (p + 1) * depth] for p in range(n)]
    names = list(range(n))
    for bit in bits:
        keep = [i for i, p in enumerate(names) if not p & bit]
        give = [names.index(names[i] ^ bit) for i in keep]
        there = flip(jnp.concatenate([blocks[i] for i in give], 0).astype(BF16), bit)
        blocks = [
            blocks[i] + there[j * depth : (j + 1) * depth].astype(F32) for j, i in enumerate(keep)
        ]
        names = [names[i] for i in keep]
    return blocks[0]


def scatter_line(own, below, above, far):
    half = own.shape[0] // 2
    low = far.astype(BF16)
    first = shift(low[:half], 1)
    second = shift(low[half:], -1)
    above = jnp.concatenate([above[:half] + first.astype(F32), above[half:]], 0).astype(BF16)
    below = jnp.concatenate([below[:half], below[half:] + second.astype(F32)], 0).astype(BF16)
    return own + shift(above, 1).astype(F32) + shift(below, -1).astype(F32)


def scatter_grad(grad_a, grad_b, core):
    bits = chip_bits()
    got_a = scatter_chips(grad_a, bits[::-1])
    got_b = scatter_chips(grad_b, bits)
    half = got_a.shape[1] // 2
    piece = scatter_line(got_a[:, :half], got_a[:, half:], got_b[:, :half], got_b[:, half:])
    return from_piece(piece, core)


def exchange_sum(make_part, own_rows):
    there = swap(make_part(True))
    return make_part(False) + there


def inverse_of(slots):
    count = slots.shape[0]
    marks = jnp.arange(count, dtype=jnp.int32)
    hit = slots[None, :] == marks[:, None]
    return jnp.sum(jnp.where(hit, marks[None, :], 0), axis=1)


def normalize(values):
    center = values - jnp.mean(values, axis=-1, keepdims=True)
    spread = jnp.mean(center * center, axis=-1, keepdims=True)
    inverse = lax.rsqrt(spread + 1e-05)
    return center * inverse, inverse


def norm_back(grad, normed, inverse, gain):
    scaled = grad * gain
    mean_one = jnp.mean(scaled, axis=-1, keepdims=True)
    mean_two = jnp.mean(scaled * normed, axis=-1, keepdims=True)
    return inverse * (scaled - mean_one - normed * mean_two)


def nn(x, y):
    return jnp.dot(x, y, preferred_element_type=F32)


def nt(x, y):
    return lax.dot_general(x, y, (((1,), (1,)), ((), ())), preferred_element_type=F32)


def tn(x, y):
    return lax.dot_general(x, y, (((0,), (0,)), ((), ())), preferred_element_type=F32)


def gelu_both(z):
    gate = 0.5 * (1.0 + lax.erf(z * 0.7071067811865476))
    slope = gate + z * jnp.exp(-0.5 * z * z) * 0.3989422804014327
    return z * gate, slope


def masked_scores(queries, key_rows, allowed, scale):
    raw = jnp.einsum("qhd,khd->hqk", queries, key_rows, preferred_element_type=F32) * scale
    return jnp.where(allowed[None], raw, -1e30)


def on_device(
    tokens,
    cotangent,
    deal,
    source,
    lengths,
    qkv_weight,
    query_bias,
    value_bias,
    out_weight,
    out_bias,
    first_gain,
    first_shift,
    up_weight,
    up_bias,
    down_weight,
    down_bias,
    second_gain,
    second_shift,
):
    core = lax.axis_index("core")
    line = lax.axis_index("tensor")
    split_ways = lax.axis_size("tensor")
    chips = lax.axis_size("chip")
    data_ways = 2 * chips
    rows, width = tokens.shape
    per_peer = rows // data_ways
    group_rows = split_ways * rows
    quarter = rows // MB
    local_width = qkv_weight.shape[2]
    local_hidden = up_weight.shape[1]
    scale = DH ** (-0.5)
    dp = ("chip", "core")

    targets = deal // group_rows
    one_hot = (targets[:, None] == jnp.arange(data_ways, dtype=jnp.int32)[None, :]).astype(
        jnp.int32
    )
    send_slot = targets * per_peer + jnp.sum(one_hot * jnp.cumsum(one_hot, axis=0), axis=1) - 1
    senders = source // group_rows
    earlier = (senders[:, None] == senders[None, :]) & (source[None, :] < source[:, None])
    recv_slot = senders * per_peer + jnp.sum(earlier.astype(jnp.int32), axis=1)
    odd = line % 2
    first_rows = lax.dynamic_slice_in_dim(recv_slot, odd * quarter, quarter)
    second_rows = lax.dynamic_slice_in_dim(recv_slot, (1 - odd) * quarter, quarter)
    recv_order = jnp.concatenate([first_rows, second_rows])
    send_order = inverse_of(send_slot)
    back_order = inverse_of(recv_order)

    def moves(which):
        pairs = []
        for k in range(2):
            for t in range(split_ways):
                m = t % 2 if which == 0 else 1 - t % 2
                pairs.append((k * split_ways + t, (t // 2) * split_ways + 2 * k + m))
        return pairs

    def to_owner(x):
        outgoing = x[send_order]
        arrived = lax.all_to_all(outgoing, dp, split_axis=0, concat_axis=0, tiled=True)
        work = relative(arrived[recv_order], 1)
        return jnp.concatenate(
            [
                lax.ppermute(work[:quarter], ("core", "tensor"), moves(0)),
                lax.ppermute(work[quarter:], ("core", "tensor"), moves(1)),
            ],
            0,
        )

    def from_owner(x):
        back = [[(b, a) for a, b in moves(which)] for which in range(2)]
        work = jnp.concatenate(
            [
                lax.ppermute(x[:quarter], ("core", "tensor"), back[0]),
                lax.ppermute(x[quarter:], ("core", "tensor"), back[1]),
            ],
            0,
        )
        outgoing = relative(work, 1)[back_order]
        arrived = lax.all_to_all(outgoing, dp, split_axis=0, concat_axis=0, tiled=True)
        return arrived[send_slot]

    rows_x = to_owner(tokens)

    which_group = line // 2
    lengths_here = pick(core == which_group, lengths[0], swap(lengths[0]))
    seq_ends = jnp.cumsum(lax.dynamic_index_in_dim(lengths_here, odd, 0, keepdims=False))
    steps = jnp.arange(quarter, dtype=jnp.int32)
    positions = jnp.concatenate(
        [
            (2 * c + b) * quarter + steps
            for c in (core, 1 - core)
            for b in (odd, 1 - odd)
        ]
    )
    seq_ids = jnp.sum((positions[:, None] >= seq_ends[None, :]).astype(jnp.int32), axis=1)
    allowed = seq_ids[:, None] == seq_ids[None, :]

    depth = qkv_weight.shape[1]
    qkv_pieces = [to_piece(qkv_weight[i], core) for i in range(3)]
    qkv_a, qkv_b = gather_weight(jnp.concatenate(qkv_pieces, 1))
    out_a, out_b = gather_weight(to_piece(out_weight.T, core))
    up_a, up_b = gather_weight(to_piece(up_weight, core))
    down_a, down_b = gather_weight(to_piece(down_weight.T, core))
    qkv_w = jnp.concatenate([qkv_a, qkv_b], 1)
    out_w = jnp.concatenate([out_a, out_b], 1)

    positions_on_line = [(line + step) % split_ways for step in (0, -1, 1, 2)]

    def bias_units(vector, unit):
        half = unit // 2
        return [
            lax.dynamic_slice_in_dim(vector, where * unit + core * half, half)
            for where in positions_on_line
        ]

    def place_units(parts, unit):
        half = unit // 2
        out = jnp.zeros((unit * split_ways,), F32)
        for where, part in zip(positions_on_line, parts):
            out = lax.dynamic_update_slice_in_dim(out, part, where * unit + core * half, 0)
        return out

    query_units = bias_units(query_bias.astype(F32), local_width)
    value_units = bias_units(value_bias.astype(F32), local_width)
    up_local = jnp.concatenate(bias_units(up_bias.astype(F32), local_hidden))
    zero_unit = jnp.zeros_like(query_units[0])
    qkv_bias = jnp.concatenate(
        [part for q, v in zip(query_units, value_units) for part in (q, zero_unit, v)]
    )
    out_bias_f, first_gain_f, first_shift_f, down_bias_f, second_gain_f, second_shift_f = (
        relative(v.astype(F32), 0)
        for v in (out_bias, first_gain, first_shift, down_bias, second_gain, second_shift)
    )

    pair_x = jnp.concatenate([rows_x, swap(rows_x)], 0)
    projected = (nn(pair_x, qkv_w) + qkv_bias).astype(BF16)
    unit = local_width // 2
    count = projected.shape[0]
    heads = split_ways * unit // DH

    def heads_of(which):
        parts = [
            projected[:, (3 * u + which) * unit : (3 * u + which + 1) * unit]
            for u in range(split_ways)
        ]
        return jnp.concatenate(parts, 1).reshape(count, heads, DH)

    queries, key_rows, value_rows = heads_of(0), heads_of(1), heads_of(2)
    scores = masked_scores(queries, key_rows, allowed, scale)
    row_max = jnp.max(scores, axis=-1, keepdims=True)
    log_total = row_max + jnp.log(jnp.sum(jnp.exp(scores - row_max), axis=-1, keepdims=True))
    probs_low = jnp.exp(scores - log_total).astype(BF16)
    mixed = (
        jnp.einsum("hqk,khd->qhd", probs_low, value_rows, preferred_element_type=F32)
        .astype(BF16)
        .reshape(count, heads * DH)
    )
    first_sum = rows_x.astype(F32) + exchange_sum(
        lambda other: nt(mixed[rows:] if other else mixed[:rows], out_w), rows
    ) + out_bias_f
    first_normed, first_inverse = normalize(first_sum)
    first_out = first_normed * first_gain_f + first_shift_f
    first_low = first_out.astype(BF16)
    pair_y = jnp.concatenate([first_low, swap(first_low)], 0)
    hidden, slope = [], []
    half_hidden = up_a.shape[1]
    for i, w in enumerate((up_a, up_b)):
        z = nn(pair_y, w) + up_local[i * half_hidden : (i + 1) * half_hidden]
        u, s = gelu_both(z)
        hidden.append(u.astype(BF16))
        slope.append(s)

    def down_part(other):
        where = slice(rows, None) if other else slice(0, rows)
        return nt(hidden[0][where], down_a) + nt(hidden[1][where], down_b)

    second_sum = first_out + exchange_sum(down_part, rows) + down_bias_f
    second_normed, second_inverse = normalize(second_sum)
    result = (second_normed * second_gain_f + second_shift_f).astype(BF16)

    rows_g = to_owner(cotangent).astype(F32)
    second_back = norm_back(rows_g, second_normed, second_inverse, second_gain_f)
    second_gain_grad = jnp.sum(rows_g * second_normed, axis=0)
    second_shift_grad = jnp.sum(rows_g, axis=0)
    down_bias_grad = jnp.sum(second_back, axis=0)
    second_low = second_back.astype(BF16)
    pair_m = jnp.concatenate([second_low, swap(second_low)], 0)
    down_grad_t = scatter_grad(tn(pair_m, hidden[0]), tn(pair_m, hidden[1]), core)
    pre_low, up_bias_parts = [], []
    for w, s in zip((down_a, down_b), slope):
        pre = nn(pair_m, w) * s
        up_bias_parts.append(jnp.sum(pre, axis=0))
        pre_low.append(pre.astype(BF16))
    up_grad = scatter_grad(tn(pair_y, pre_low[0]), tn(pair_y, pre_low[1]), core)

    def up_part(other):
        where = slice(rows, None) if other else slice(0, rows)
        return nt(pre_low[0][where], up_a) + nt(pre_low[1][where], up_b)

    first_grad = second_back + exchange_sum(up_part, rows)
    first_back = norm_back(first_grad, first_normed, first_inverse, first_gain_f)
    first_gain_grad = jnp.sum(first_grad * first_normed, axis=0)
    first_shift_grad = jnp.sum(first_grad, axis=0)
    out_bias_grad = jnp.sum(first_back, axis=0)
    first_back_low = first_back.astype(BF16)
    pair_o = jnp.concatenate([first_back_low, swap(first_back_low)], 0)
    out_half = out_a.shape[1]
    out_grad = tn(pair_o, mixed)
    out_grad_t = scatter_grad(out_grad[:, :out_half], out_grad[:, out_half:], core)
    mixed_back = nn(pair_o, out_w).astype(BF16).reshape(count, heads, DH)
    value_back = jnp.einsum(
        "hqk,qhd->khd", probs_low, mixed_back, preferred_element_type=F32
    ).reshape(count, heads * DH)
    prob_back = jnp.einsum(
        "qhd,khd->hqk", mixed_back, value_rows, preferred_element_type=F32
    )
    again = masked_scores(queries, key_rows, allowed, scale)
    probs = jnp.exp(again - log_total)
    row_dot = jnp.sum(prob_back * probs, axis=-1, keepdims=True)
    score_back = (probs * (prob_back - row_dot) * scale).astype(BF16)
    query_back = jnp.einsum(
        "hqk,khd->qhd", score_back, key_rows, preferred_element_type=F32
    ).reshape(count, heads * DH)
    key_back = jnp.einsum(
        "hqk,qhd->khd", score_back, queries, preferred_element_type=F32
    ).reshape(count, heads * DH)
    query_bias_local = jnp.sum(query_back, axis=0)
    value_bias_local = jnp.sum(value_back, axis=0)
    back_parts = []
    for u in range(split_ways):
        for part in (query_back, key_back, value_back):
            back_parts.append(part[:, u * unit : (u + 1) * unit].astype(BF16))
    proj_back = jnp.concatenate(back_parts, 1)
    qkv_half = qkv_a.shape[1]
    qkv_grad_w = tn(pair_x, proj_back)
    qkv_piece = scatter_grad_piece(qkv_grad_w[:, :qkv_half], qkv_grad_w[:, qkv_half:])
    qkv_grad = jnp.stack(
        [from_piece(qkv_piece[:, i * unit : (i + 1) * unit], core) for i in range(3)]
    )
    input_back = first_back + exchange_sum(
        lambda other: nt(proj_back[rows:] if other else proj_back[:rows], qkv_w), rows
    )

    layer_out = from_owner(result)
    tokens_grad = from_owner(input_back.astype(BF16)).astype(F32)

    units = lambda v, n: [v[i * n : (i + 1) * n] for i in range(split_ways)]
    feature = [
        relative(v, 0)
        for v in (
            out_bias_grad,
            first_gain_grad,
            first_shift_grad,
            down_bias_grad,
            second_gain_grad,
            second_shift_grad,
        )
    ]
    placed = [
        place_units(units(query_bias_local, unit), local_width),
        place_units(units(value_bias_local, unit), local_width),
        place_units(units(jnp.concatenate(up_bias_parts), local_hidden // 2), local_hidden),
    ]
    packed = jnp.concatenate(feature + placed).reshape(-1, 128)
    packed = packed + swap(packed)
    for bit in chip_bits():
        packed = packed + flip(packed, bit)
    step = 1
    while step < split_ways:
        packed = packed + lax.ppermute(
            packed, "tensor", [(i, i ^ step) for i in range(split_ways)]
        )
        step *= 2
    packed = packed.reshape(-1)
    sizes = [v.shape[0] for v in feature + placed]
    ends = [sum(sizes[: i + 1]) for i in range(len(sizes))]
    (
        out_bias_grad,
        first_gain_grad,
        first_shift_grad,
        down_bias_grad,
        second_gain_grad,
        second_shift_grad,
        query_bias_grad,
        value_bias_grad,
        up_bias_grad,
    ) = (packed[end - size : end] for end, size in zip(ends, sizes))
    return (
        layer_out,
        tokens_grad,
        qkv_grad,
        query_bias_grad,
        value_bias_grad,
        out_grad_t.T,
        out_bias_grad,
        first_gain_grad,
        first_shift_grad,
        up_grad,
        up_bias_grad,
        down_grad_t.T,
        down_bias_grad,
        second_gain_grad,
        second_shift_grad,
    )


def scatter_grad_piece(grad_a, grad_b):
    bits = chip_bits()
    got_a = scatter_chips(grad_a, bits[::-1])
    got_b = scatter_chips(grad_b, bits)
    half = got_a.shape[1] // 2
    return scatter_line(got_a[:, :half], got_a[:, half:], got_b[:, :half], got_b[:, half:])


def solution(mesh):
    data_ways, split_ways = mesh.shape["dp"], mesh.shape["tensor"]
    fine = Mesh(mesh.devices.reshape(data_ways // 2, 2, split_ways), ALL)
    dp = ("chip", "core")
    in_specs = (
        P(ALL, None),
        P(ALL, None),
        P(ALL),
        P(ALL),
        P(dp, None, None),
        P(None, dp, "tensor"),
        P(),
        P(),
        P("tensor", dp),
        P(),
        P(),
        P(),
        P(dp, "tensor"),
        P(),
        P("tensor", dp),
        P(),
        P(),
        P(),
    )
    out_specs = (
        P(ALL, None),
        P(ALL, None),
        P(None, dp, "tensor"),
        P(),
        P(),
        P("tensor", dp),
        P(),
        P(),
        P(),
        P(dp, "tensor"),
        P(),
        P("tensor", dp),
        P(),
        P(),
        P(),
    )
    return jax.shard_map(
        on_device, mesh=fine, in_specs=in_specs, out_specs=out_specs, check_vma=False
    )
```

```python
import functools

import jax
import jax.numpy as jnp
from jax import lax
from jax.experimental import pallas as pl
from jax.experimental.pallas import tpu as pltpu
from jax.sharding import Mesh, PartitionSpec as P

DH = 64
MB = 2
F32 = jnp.float32
BF16 = jnp.bfloat16
ALL = ("chip", "core", "tensor")
MESH = pl.DeviceIdType.MESH
ANY = pl.BlockSpec(memory_space=pl.ANY)
IN_VMEM = pl.BlockSpec(memory_space=pltpu.VMEM)


def swap(x):
    return lax.ppermute(x, "core", [(0, 1), (1, 0)])


def flip(x, bit):
    n = lax.axis_size("chip")
    return lax.ppermute(x, "chip", [(i, i ^ bit) for i in range(n)])


def chip_bits():
    n = lax.axis_size("chip")
    return [1 << i for i in range(n.bit_length() - 1)]


class Place:
    def __init__(self, chips, ways):
        self.chip = lax.axis_index("chip")
        self.core = lax.axis_index("core")
        self.line = lax.axis_index("tensor")
        self.ways = ways
        self.count = chips.bit_length() - 1
        self.bits = [lax.rem(self.chip // (1 << i), 2) for i in range(self.count)]

    def other_core(self):
        return {"core": 1 - self.core}

    def along(self, step):
        return {"tensor": lax.rem(self.line + step + self.ways, self.ways)}

    def across(self, i):
        return {"chip": self.chip + (1 - 2 * self.bits[i]) * (1 << i)}

    def unit(self, step):
        return lax.rem(self.line + step + self.ways, self.ways)

    def greet(self):
        barrier = pltpu.get_barrier_semaphore()
        partners = [self.other_core(), self.along(1), self.along(-1)]
        partners += [self.across(i) for i in range(self.count)]
        for partner in partners:
            pl.semaphore_signal(barrier, inc=1, device_id=partner, device_id_type=MESH)
        pl.semaphore_wait(barrier, len(partners))

    def blocks(self, free, flipped=None):
        index = []
        for i in reversed(range(self.count)):
            if i in free:
                index.append(slice(None))
            elif i == flipped:
                index.append(1 - self.bits[i])
            else:
                index.append(self.bits[i])
        return tuple(index)


UNITS = (0, -1, 1, 2)


def unit_bits(u, count):
    order = list(range(count))
    return order if u in (0, 3) else order[::-1]


def remote(src, dst, send, recv, where):
    return pltpu.make_async_remote_copy(
        src_ref=src,
        dst_ref=dst,
        send_sem=send,
        recv_sem=recv,
        device_id=where,
        device_id_type=MESH,
    )


def columns(index, width):
    return pl.ds(pl.multiple_of(index * width, width), width)


def row_span(index, depth):
    return pl.ds(pl.multiple_of(index * depth, depth), depth)


class Gather:
    def __init__(self, place, shard, whole, piece, sends, recvs, own_sem):
        self.place, self.shard, self.whole, self.piece = place, shard, whole, piece
        self.sends, self.recvs, self.own_sem = sends, recvs, own_sem
        self.width = piece.shape[1]
        self.depth = shard.shape[0]
        self.copies = []

    def slot(self, u):
        return columns(self.place.unit(UNITS[u]), self.width)

    def launch(self, number, src, dst, where):
        copy = remote(src, dst, self.sends.at[number], self.recvs.at[number], where)
        copy.start()
        self.copies.append(copy)
        return copy

    def pair(self):
        p = self.place
        mine = row_span(p.core, self.depth)
        self.keep = pltpu.make_async_copy(
            self.shard.at[:, columns(p.core, self.width)], self.piece.at[mine], self.own_sem.at[0]
        )
        self.keep.start()
        self.pair_copy = self.launch(
            0, self.shard.at[:, columns(1 - p.core, self.width)], self.piece.at[mine], p.other_core()
        )

    def open(self):
        p = self.place
        self.keep.wait()
        self.pair_copy.wait_recv()
        here = self.whole.at[p.blocks(()) + (slice(None), self.slot(0))]
        self.settle = pltpu.make_async_copy(self.piece, here, self.own_sem.at[1])
        self.settle.start()
        self.below = self.launch(1, self.piece, here, p.along(1))
        self.above = self.launch(2, self.piece, here, p.along(-1))
        self.stages = [[None] * p.count for _ in range(4)]
        self.across(0, 0, self.piece)

    def across(self, u, stage, src=None):
        p = self.place
        if p.count == 0:
            return
        order = unit_bits(u, p.count)
        where = self.whole.at[p.blocks(order[:stage]) + (slice(None), self.slot(u))]
        self.stages[u][stage] = self.launch(
            5 + u * p.count + stage,
            where if src is None else src,
            where,
            p.across(order[stage]),
        )

    def half(self, u, part):
        rows = pl.ds(part * self.depth, self.depth)
        return self.whole.at[self.place.blocks(()) + (rows, self.slot(u))]

    def line_below(self):
        self.below.wait_recv()
        self.far_low = self.launch(3, self.half(1, 0), self.half(1, 0), self.place.along(1))
        self.across(1, 0)

    def line_above(self):
        self.above.wait_recv()
        self.far_high = self.launch(4, self.half(2, 1), self.half(2, 1), self.place.along(-1))
        self.across(2, 0)

    def line_far(self):
        self.far_low.wait_recv()
        self.far_high.wait_recv()
        self.across(3, 0)

    def forward(self, u, stage):
        self.stages[u][stage - 1].wait_recv()
        if u == 0 and stage == 1:
            self.settle.wait()
        self.across(u, stage)

    def finish(self):
        if self.place.count < 2:
            self.settle.wait()
        for u in range(4):
            if self.place.count:
                self.stages[u][-1].wait_recv()
        for copy in self.copies:
            copy.wait_send()


def gather_steps(works, count):
    steps = []
    for w in works:
        steps.append(w.pair)
    for w in works:
        steps.append(w.open)
    for w in works:
        steps.append(w.line_below)
        steps.append(w.line_above)
    for stage in range(1, count):
        for u in (0, 1, 2):
            for w in works:
                if stage == 1 and u == 1:
                    steps.append(w.line_far)
                steps.append(functools.partial(w.forward, u, stage))
    if count < 2:
        for w in works:
            steps.append(w.line_far)
    for stage in range(1, count):
        for w in works:
            steps.append(functools.partial(w.forward, 3, stage))
    for w in works:
        steps.append(w.finish)
    return steps


def gather_kernel(chips, ways, number, *refs):
    place = Place(chips, ways)
    shards, refs = refs[:number], refs[number:]
    wholes, refs = refs[:number], refs[number:]
    pieces, refs = refs[:number], refs[number:]
    sends, recvs, own = refs
    place.greet()
    works = [
        Gather(place, shards[i], wholes[i], pieces[i], sends.at[i], recvs.at[i], own.at[i])
        for i in range(number)
    ]
    for step in gather_steps(works, place.count):
        step()


def gather_weights(shards, chips, ways, collective_id):
    bits = chips.bit_length() - 1
    number = len(shards)
    sems = 5 + 4 * bits
    wholes = pl.pallas_call(
        functools.partial(gather_kernel, chips, ways, number),
        in_specs=[ANY] * number,
        out_specs=[ANY] * number,
        out_shape=[
            jax.ShapeDtypeStruct(
                (2,) * bits + (2 * s.shape[0], ways * s.shape[1] // 2), s.dtype
            )
            for s in shards
        ],
        scratch_shapes=[
            pltpu.VMEM((2 * s.shape[0], s.shape[1] // 2), s.dtype) for s in shards
        ]
        + [
            pltpu.SemaphoreType.DMA((number, sems)),
            pltpu.SemaphoreType.DMA((number, sems)),
            pltpu.SemaphoreType.DMA((number, 2)),
        ],
        name="gather_weights",
        compiler_params=pltpu.CompilerParams(
            collective_id=collective_id, has_side_effects=True, vmem_limit_bytes=32 << 20
        ),
    )(*shards)
    return [w.reshape(-1, w.shape[-1]) for w in wholes]


class Scatter:
    def __init__(self, place, whole, shard, mine, slots, temps, keeps, line, last, sems):
        self.place, self.whole, self.shard = place, whole, shard
        self.mine, self.slots, self.temps, self.keeps = mine, slots, temps, keeps
        self.line_in, self.line_out, self.final = line
        self.far_in = last
        self.sends, self.recvs, self.own = sems
        self.width = shard.shape[1] // 2
        self.depth = shard.shape[0]
        self.copies = []
        self.stages = [[None] * place.count for _ in range(4)]

    def launch(self, number, src, dst, where):
        copy = remote(src, dst, self.sends.at[number], self.recvs.at[number], where)
        copy.start()
        self.copies.append(copy)
        return copy

    def slot(self, u):
        return columns(self.place.unit(UNITS[u]), self.width)

    def open(self, u):
        p = self.place
        order = unit_bits(u, p.count)
        first = order[0]
        lanes = (slice(None), self.slot(u))
        self.stages[u][0] = self.launch(
            u * p.count,
            self.whole.at[p.blocks(order[1:], first) + lanes],
            self.slots[0].at[u],
            p.across(first),
        )
        copy = pltpu.make_async_copy(
            self.whole.at[p.blocks(order[1:]) + lanes], self.mine.at[u], self.own.at[u]
        )
        copy.start()
        self.stages[u].append(copy)

    def chip_index(self, u, stage, other):
        p = self.place
        order = unit_bits(u, p.count)
        left = order[stage:]
        index = []
        for i in sorted(left, reverse=True):
            if i == left[0]:
                index.append(1 - p.bits[i] if other else p.bits[i])
            else:
                index.append(slice(None))
        return tuple(index)

    def forward(self, u, stage):
        p = self.place
        order = unit_bits(u, p.count)
        self.stages[u][stage - 1].wait_recv()
        if stage == 1:
            self.stages[u][-1].wait()
        source = self.mine if stage == 1 else self.keeps[stage - 1]
        there = (u,) + self.chip_index(u, stage, True)
        here = (u,) + self.chip_index(u, stage, False)
        arrived = self.slots[stage - 1]
        self.temps[stage - 1][u] = (
            source[there].astype(F32) + arrived[there].astype(F32)
        ).astype(BF16)
        self.stages[u][stage] = self.launch(
            u * p.count + stage,
            self.temps[stage - 1].at[u],
            self.slots[stage].at[u],
            p.across(order[stage]),
        )
        self.keeps[stage][u] = source[here].astype(F32) + arrived[here].astype(F32)

    def total(self, u):
        p = self.place
        last = p.count - 1
        self.stages[u][last].wait_recv()
        if last == 0:
            self.stages[u][-1].wait()
            return self.mine[u].astype(F32) + self.slots[0][u].astype(F32)
        return self.keeps[last][u] + self.slots[last][u].astype(F32)

    def line_far(self):
        p = self.place
        base = 4 * p.count
        self.far_in[0] = self.total(3).astype(BF16)
        low, high = pl.ds(0, self.depth), pl.ds(self.depth, self.depth)
        self.low = self.launch(
            base, self.far_in.at[0, low], self.far_in.at[1, low], p.along(1)
        )
        self.high = self.launch(
            base + 1, self.far_in.at[0, high], self.far_in.at[1, high], p.along(-1)
        )

    def line_above(self):
        p = self.place
        base = 4 * p.count
        depth = self.depth
        total = self.total(2)
        self.low.wait_recv()
        self.line_out[0, :depth] = (total[:depth] + self.far_in[1, :depth].astype(F32)).astype(
            BF16
        )
        self.line_out[0, depth:] = total[depth:].astype(BF16)
        self.from_below = self.launch(
            base + 2, self.line_out.at[0], self.line_in.at[0], p.along(1)
        )

    def line_below(self):
        p = self.place
        base = 4 * p.count
        depth = self.depth
        total = self.total(1)
        self.high.wait_recv()
        self.line_out[1, depth:] = (total[depth:] + self.far_in[1, depth:].astype(F32)).astype(
            BF16
        )
        self.line_out[1, :depth] = total[:depth].astype(BF16)
        self.from_above = self.launch(
            base + 3, self.line_out.at[1], self.line_in.at[1], p.along(-1)
        )

    def close(self):
        p = self.place
        total = self.total(0)
        self.from_below.wait_recv()
        self.from_above.wait_recv()
        self.final[...] = total + self.line_in[0].astype(F32) + self.line_in[1].astype(F32)
        lanes = columns(p.core, self.width)
        self.pair = self.launch(
            4 * p.count + 4,
            self.final.at[row_span(1 - p.core, self.depth)],
            self.shard.at[:, lanes],
            p.other_core(),
        )
        self.keep = pltpu.make_async_copy(
            self.final.at[row_span(p.core, self.depth)], self.shard.at[:, lanes], self.own.at[4]
        )
        self.keep.start()

    def finish(self):
        self.keep.wait()
        self.pair.wait_recv()
        for copy in self.copies:
            copy.wait_send()


def scatter_steps(works, count):
    steps = []
    for u in (3, 2, 1, 0):
        for w in works:
            steps.append(functools.partial(w.open, u))
    for stage in range(1, count):
        for u in (3, 2, 1, 0):
            for w in works:
                steps.append(functools.partial(w.forward, u, stage))
    for name in ("line_far", "line_above", "line_below", "close", "finish"):
        for w in works:
            steps.append(getattr(w, name))
    return steps


def scatter_scratch(depth, width, bits):
    shapes = []
    for stage in range(bits):
        left = (2,) * (bits - 1 - stage)
        shapes.append(pltpu.VMEM((4,) + left + (2 * depth, width), BF16))
    shapes.append(pltpu.VMEM((4,) + (2,) * (bits - 1) + (2 * depth, width), BF16))
    for stage in range(1, bits):
        left = (2,) * (bits - 1 - stage)
        shapes.append(pltpu.VMEM((4,) + left + (2 * depth, width), BF16))
        shapes.append(pltpu.VMEM((4,) + left + (2 * depth, width), F32))
    shapes.append(pltpu.VMEM((2, 2 * depth, width), BF16))
    shapes.append(pltpu.VMEM((2, 2 * depth, width), BF16))
    shapes.append(pltpu.VMEM((2, 2 * depth, width), BF16))
    shapes.append(pltpu.VMEM((2 * depth, width), F32))
    return shapes


def scatter_work(place, whole, shard, scratch, sems):
    count = place.count
    scratch = list(scratch)
    slots = [scratch.pop(0) for _ in range(count)]
    mine = scratch.pop(0)
    temps, keeps = [], [None]
    for _ in range(1, count):
        temps.append(scratch.pop(0))
        keeps.append(scratch.pop(0))
    line_in, line_out, far_in, final = scratch
    return Scatter(
        place, whole, shard, mine, slots, temps, keeps, (line_in, line_out, final), far_in, sems
    )


def scatter_kernel(chips, ways, number, *refs):
    place = Place(chips, ways)
    wholes, refs = refs[:number], refs[number:]
    shards, refs = refs[:number], refs[number:]
    sends, recvs, own = refs[-3:]
    each = (len(refs) - 3) // number
    place.greet()
    works = [
        scatter_work(
            place,
            wholes[i],
            shards[i],
            refs[i * each : (i + 1) * each],
            (sends.at[i], recvs.at[i], own.at[i]),
        )
        for i in range(number)
    ]
    for step in scatter_steps(works, place.count):
        step()


def scatter_grads(grads, chips, ways, collective_id):
    bits = chips.bit_length() - 1
    number = len(grads)
    shapes = [(g.shape[0] // (2 * chips), g.shape[1] // ways) for g in grads]
    scratch = []
    for depth, width in shapes:
        scratch += scatter_scratch(depth, width, bits)
    sems = 4 * bits + 5
    return pl.pallas_call(
        functools.partial(scatter_kernel, chips, ways, number),
        in_specs=[ANY] * number,
        out_specs=[ANY] * number,
        out_shape=[jax.ShapeDtypeStruct((depth, 2 * width), F32) for depth, width in shapes],
        scratch_shapes=scratch
        + [
            pltpu.SemaphoreType.DMA((number, sems)),
            pltpu.SemaphoreType.DMA((number, sems)),
            pltpu.SemaphoreType.DMA((number, 5)),
        ],
        name="scatter_grads",
        compiler_params=pltpu.CompilerParams(
            collective_id=collective_id, has_side_effects=True, vmem_limit_bytes=48 << 20
        ),
    )(
        *[
            g.reshape((2,) * bits + (2 * depth, g.shape[1]))
            for g, (depth, _) in zip(grads, shapes)
        ]
    )


def head_lanes(shape, h):
    lanes = lax.broadcasted_iota(jnp.int32, shape, 1)
    return (lanes // DH) == h


def attention_forward_kernel(qkv_ref, col_ref, row_ref, o_ref, lse_ref, vt_ref):
    k = qkv_ref[:, 128:256]
    vt_ref[...] = qkv_ref[:, 256:384].astype(F32).T.astype(BF16)
    q = qkv_ref[:, 0:128] * jnp.asarray(DH**-0.5, BF16)
    same = col_ref[...] == row_ref[...]
    outs = []
    for h in range(2):
        q_h = jnp.where(head_lanes(q.shape, h), q, jnp.zeros_like(q))
        s = jnp.where(same, nt(k, q_h), -1e30)
        top = jnp.max(s, axis=0, keepdims=True)
        p = jnp.exp(s - top)
        total = jnp.sum(p, axis=0, keepdims=True)
        low = (p * (1.0 / total)).astype(BF16)
        outs.append(nn(vt_ref[h * DH : (h + 1) * DH], low))
        lse_ref[0, h : h + 1, :] = top + jnp.log(total)
    o_ref[...] = jnp.concatenate(outs, 0).T.astype(BF16)


def attention_forward(qkv, seq):
    count = qkv.shape[0]
    pairs = qkv.shape[1] // 384
    return pl.pallas_call(
        attention_forward_kernel,
        grid=(pairs,),
        in_specs=[
            pl.BlockSpec((count, 384), lambda p: (0, p)),
            pl.BlockSpec((count, 1), lambda p: (0, 0)),
            pl.BlockSpec((1, count), lambda p: (0, 0)),
        ],
        out_specs=[
            pl.BlockSpec((count, 128), lambda p: (0, p)),
            pl.BlockSpec((1, 2, count), lambda p: (p, 0, 0)),
        ],
        out_shape=[
            jax.ShapeDtypeStruct((count, pairs * 128), BF16),
            jax.ShapeDtypeStruct((pairs, 2, count), F32),
        ],
        scratch_shapes=[pltpu.VMEM((128, count), BF16)],
        name="attention_forward",
        cost_estimate=pl.CostEstimate(
            flops=pairs * 2 * 4 * count * count * 256,
            bytes_accessed=qkv.size * 2 + count * pairs * 256,
            transcendentals=pairs * 2 * count * count,
        ),
        compiler_params=pltpu.CompilerParams(
            dimension_semantics=("arbitrary",), vmem_limit_bytes=56 << 20
        ),
    )(qkv, seq[:, None], seq[None, :])


def attention_backward_kernel(
    qkv_ref, do_ref, lse_ref, col_ref, row_ref, dqkv_ref, qb_ref, vb_ref, kt_ref
):
    k = qkv_ref[:, 128:256]
    v = qkv_ref[:, 256:384]
    kt_ref[...] = k.astype(F32).T.astype(BF16)
    q = qkv_ref[:, 0:128] * jnp.asarray(DH**-0.5, BF16)
    do = do_ref[...]
    same = col_ref[...] == row_ref[...]
    dq_t, dk, dv = [], None, None
    for h in range(2):
        keep = head_lanes(q.shape, h)
        q_h = jnp.where(keep, q, jnp.zeros_like(q))
        do_h = jnp.where(keep, do, jnp.zeros_like(do))
        s_t = jnp.where(same, nt(k, q_h), -1e30)
        p_t = jnp.exp(s_t - lse_ref[0, h : h + 1, :])
        dp_t = nt(v, do_h)
        delta = jnp.sum(dp_t * p_t, axis=0, keepdims=True)
        dv_h = nn(p_t.astype(BF16), do_h)
        ds_t = (p_t * (dp_t - delta)).astype(BF16)
        dk_h = nn(ds_t, q_h)
        dq_t.append(nn(kt_ref[h * DH : (h + 1) * DH], ds_t))
        dk = dk_h if dk is None else dk + dk_h
        dv = dv_h if dv is None else dv + dv_h
    dq = jnp.concatenate(dq_t, 0).T * (DH**-0.5)
    dqkv_ref[:, 0:128] = dq.astype(BF16)
    dqkv_ref[:, 128:256] = dk.astype(BF16)
    dqkv_ref[:, 256:384] = dv.astype(BF16)
    qb_ref[...] = jnp.broadcast_to(jnp.sum(dq, axis=0, keepdims=True)[None], qb_ref.shape)
    vb_ref[...] = jnp.broadcast_to(jnp.sum(dv, axis=0, keepdims=True)[None], vb_ref.shape)


def attention_backward(qkv, d_out, lse, seq):
    count = qkv.shape[0]
    pairs = qkv.shape[1] // 384
    dqkv, qb, vb = pl.pallas_call(
        attention_backward_kernel,
        grid=(pairs,),
        in_specs=[
            pl.BlockSpec((count, 384), lambda p: (0, p)),
            pl.BlockSpec((count, 128), lambda p: (0, p)),
            pl.BlockSpec((1, 2, count), lambda p: (p, 0, 0)),
            pl.BlockSpec((count, 1), lambda p: (0, 0)),
            pl.BlockSpec((1, count), lambda p: (0, 0)),
        ],
        out_specs=[
            pl.BlockSpec((count, 384), lambda p: (0, p)),
            pl.BlockSpec((1, 8, 128), lambda p: (p, 0, 0)),
            pl.BlockSpec((1, 8, 128), lambda p: (p, 0, 0)),
        ],
        out_shape=[
            jax.ShapeDtypeStruct((count, pairs * 384), BF16),
            jax.ShapeDtypeStruct((pairs, 8, 128), F32),
            jax.ShapeDtypeStruct((pairs, 8, 128), F32),
        ],
        scratch_shapes=[pltpu.VMEM((128, count), BF16)],
        name="attention_backward",
        cost_estimate=pl.CostEstimate(
            flops=pairs * 2 * 10 * count * count * 256,
            bytes_accessed=qkv.size * 4 + count * pairs * 256,
            transcendentals=pairs * 2 * count * count,
        ),
        compiler_params=pltpu.CompilerParams(
            dimension_semantics=("arbitrary",), vmem_limit_bytes=60 << 20
        ),
    )(qkv, d_out, lse, seq[:, None], seq[None, :])
    return dqkv, qb[:, 0], vb[:, 0]


def exchange_sum(make_part):
    there = swap(make_part(True))
    return make_part(False) + there


def inverse_of(slots):
    count = slots.shape[0]
    marks = jnp.arange(count, dtype=jnp.int32)
    hit = slots[None, :] == marks[:, None]
    return jnp.sum(jnp.where(hit, marks[None, :], 0), axis=1)


def normalize(values):
    center = values - jnp.mean(values, axis=-1, keepdims=True)
    spread = jnp.mean(center * center, axis=-1, keepdims=True)
    inverse = lax.rsqrt(spread + 1e-05)
    return center * inverse, inverse


def norm_back(grad, normed, inverse, gain):
    scaled = grad * gain
    mean_one = jnp.mean(scaled, axis=-1, keepdims=True)
    mean_two = jnp.mean(scaled * normed, axis=-1, keepdims=True)
    return inverse * (scaled - mean_one - normed * mean_two)


def nn(x, y):
    return jnp.dot(x, y, preferred_element_type=F32)


def nt(x, y):
    return lax.dot_general(x, y, (((1,), (1,)), ((), ())), preferred_element_type=F32)


def tn(x, y):
    return lax.dot_general(x, y, (((0,), (0,)), ((), ())), preferred_element_type=F32)


def gelu_both(z):
    gate = 0.5 * (1.0 + lax.erf(z * 0.7071067811865476))
    slope = gate + z * jnp.exp(-0.5 * z * z) * 0.3989422804014327
    return z * gate, slope


def on_device(
    tokens,
    cotangent,
    deal,
    source,
    lengths,
    qkv_weight,
    query_bias,
    value_bias,
    out_weight,
    out_bias,
    first_gain,
    first_shift,
    up_weight,
    up_bias,
    down_weight,
    down_bias,
    second_gain,
    second_shift,
):
    core = lax.axis_index("core")
    line = lax.axis_index("tensor")
    ways = lax.axis_size("tensor")
    chips = lax.axis_size("chip")
    data_ways = 2 * chips
    rows, width = tokens.shape
    per_peer = rows // data_ways
    group_rows = ways * rows
    quarter = rows // MB
    dp = ("chip", "core")

    targets = deal // group_rows
    one_hot = (targets[:, None] == jnp.arange(data_ways, dtype=jnp.int32)[None, :]).astype(
        jnp.int32
    )
    send_slot = targets * per_peer + jnp.sum(one_hot * jnp.cumsum(one_hot, axis=0), axis=1) - 1
    senders = source // group_rows
    earlier = (senders[:, None] == senders[None, :]) & (source[None, :] < source[:, None])
    recv_slot = senders * per_peer + jnp.sum(earlier.astype(jnp.int32), axis=1)
    odd = line % 2
    first_rows = lax.dynamic_slice_in_dim(recv_slot, odd * quarter, quarter)
    second_rows = lax.dynamic_slice_in_dim(recv_slot, (1 - odd) * quarter, quarter)
    recv_order = jnp.concatenate([first_rows, second_rows])
    send_order = inverse_of(send_slot)
    back_order = inverse_of(recv_order)

    def moves(which):
        pairs = []
        for k in range(2):
            for t in range(ways):
                m = t % 2 if which == 0 else 1 - t % 2
                pairs.append((k * ways + t, (t // 2) * ways + 2 * k + m))
        return pairs

    def to_owner(x):
        outgoing = x[send_order]
        arrived = lax.all_to_all(outgoing, dp, split_axis=0, concat_axis=0, tiled=True)
        work = arrived[recv_order]
        return jnp.concatenate(
            [
                lax.ppermute(work[:quarter], ("core", "tensor"), moves(0)),
                lax.ppermute(work[quarter:], ("core", "tensor"), moves(1)),
            ],
            0,
        )

    def from_owner(x):
        back = [[(b, a) for a, b in moves(which)] for which in range(2)]
        work = jnp.concatenate(
            [
                lax.ppermute(x[:quarter], ("core", "tensor"), back[0]),
                lax.ppermute(x[quarter:], ("core", "tensor"), back[1]),
            ],
            0,
        )
        outgoing = work[back_order]
        arrived = lax.all_to_all(outgoing, dp, split_axis=0, concat_axis=0, tiled=True)
        return arrived[send_slot]

    depth = qkv_weight.shape[1]
    unit = qkv_weight.shape[2] // 2
    qkv_shard = (
        qkv_weight.reshape(3, depth, 2, unit).transpose(1, 2, 0, 3).reshape(depth, 6 * unit)
    )
    (qkv_w,) = gather_weights([qkv_shard], chips, ways, 0)
    rows_x = to_owner(tokens)
    out_w, up_w, down_w = gather_weights([out_weight.T, up_weight, down_weight.T], chips, ways, 1)

    which_group = line // 2
    lengths_here = jnp.where(core == which_group, lengths[0], swap(lengths[0]))
    seq_ends = jnp.cumsum(lax.dynamic_index_in_dim(lengths_here, odd, 0, keepdims=False))
    steps = jnp.arange(quarter, dtype=jnp.int32)
    positions = jnp.concatenate(
        [(2 * c + b) * quarter + steps for c in (core, 1 - core) for b in (odd, 1 - odd)]
    )
    seq_ids = jnp.sum((positions[:, None] >= seq_ends[None, :]).astype(jnp.int32), axis=1)

    def local_half(vector):
        parts = vector.astype(F32).reshape(ways, 2, -1)
        return lax.dynamic_index_in_dim(parts, core, 1, keepdims=False)

    def placed_half(parts):
        here = jnp.arange(2)[None, :, None] == core
        return jnp.where(here, parts[:, None, :], 0.0).reshape(-1)

    query_half, value_half = local_half(query_bias), local_half(value_bias)
    qkv_bias = jnp.stack([query_half, jnp.zeros_like(query_half), value_half], 1).reshape(-1)
    up_local = local_half(up_bias).reshape(-1)
    out_bias_f, first_gain_f, first_shift_f, down_bias_f, second_gain_f, second_shift_f = (
        v.astype(F32)
        for v in (out_bias, first_gain, first_shift, down_bias, second_gain, second_shift)
    )

    pair_x = jnp.concatenate([rows_x, swap(rows_x)], 0)
    projected = (nn(pair_x, qkv_w) + qkv_bias).astype(BF16)
    mixed, lse = attention_forward(projected, seq_ids)
    first_sum = (
        rows_x.astype(F32)
        + exchange_sum(lambda other: nt(mixed[rows:] if other else mixed[:rows], out_w))
        + out_bias_f
    )
    first_normed, first_inverse = normalize(first_sum)
    first_out = first_normed * first_gain_f + first_shift_f
    first_low = first_out.astype(BF16)
    pair_y = jnp.concatenate([first_low, swap(first_low)], 0)
    hidden, slope = gelu_both(nn(pair_y, up_w) + up_local)
    hidden = hidden.astype(BF16)
    second_sum = (
        first_out
        + exchange_sum(lambda other: nt(hidden[rows:] if other else hidden[:rows], down_w))
        + down_bias_f
    )
    second_normed, second_inverse = normalize(second_sum)
    result = (second_normed * second_gain_f + second_shift_f).astype(BF16)

    rows_g = to_owner(cotangent).astype(F32)
    second_back = norm_back(rows_g, second_normed, second_inverse, second_gain_f)
    second_gain_grad = jnp.sum(rows_g * second_normed, axis=0)
    second_shift_grad = jnp.sum(rows_g, axis=0)
    down_bias_grad = jnp.sum(second_back, axis=0)
    second_low = second_back.astype(BF16)
    pair_m = jnp.concatenate([second_low, swap(second_low)], 0)
    down_grad = tn(pair_m, hidden).astype(BF16)
    pre = nn(pair_m, down_w) * slope
    up_bias_local = jnp.sum(pre, axis=0)
    pre = pre.astype(BF16)
    up_grad = tn(pair_y, pre).astype(BF16)
    first_grad = second_back + exchange_sum(
        lambda other: nt(pre[rows:] if other else pre[:rows], up_w)
    )
    down_shard, up_shard = scatter_grads([down_grad, up_grad], chips, ways, 2)
    first_back = norm_back(first_grad, first_normed, first_inverse, first_gain_f)
    first_gain_grad = jnp.sum(first_grad * first_normed, axis=0)
    first_shift_grad = jnp.sum(first_grad, axis=0)
    out_bias_grad = jnp.sum(first_back, axis=0)
    first_back_low = first_back.astype(BF16)
    pair_o = jnp.concatenate([first_back_low, swap(first_back_low)], 0)
    out_grad = tn(pair_o, mixed).astype(BF16)
    mixed_back = nn(pair_o, out_w).astype(BF16)
    proj_back, query_bias_local, value_bias_local = attention_backward(
        projected, mixed_back, lse, seq_ids
    )
    qkv_grad = tn(pair_x, proj_back).astype(BF16)
    out_shard, qkv_shard = scatter_grads([out_grad, qkv_grad], chips, ways, 3)
    input_back = first_back + exchange_sum(
        lambda other: nt(proj_back[rows:] if other else proj_back[:rows], qkv_w)
    )

    layer_out = from_owner(result)
    tokens_grad = from_owner(input_back.astype(BF16)).astype(F32)

    feature = [
        out_bias_grad,
        first_gain_grad,
        first_shift_grad,
        down_bias_grad,
        second_gain_grad,
        second_shift_grad,
    ]
    placed = [
        placed_half(query_bias_local),
        placed_half(value_bias_local),
        placed_half(up_bias_local.reshape(ways, -1)),
    ]
    packed = jnp.concatenate(feature + placed).reshape(-1, 128)
    packed = packed + swap(packed)
    for bit in chip_bits():
        packed = packed + flip(packed, bit)
    step = 1
    while step < ways:
        packed = packed + lax.ppermute(packed, "tensor", [(i, i ^ step) for i in range(ways)])
        step *= 2
    packed = packed.reshape(-1)
    sizes = [v.shape[0] for v in feature + placed]
    ends = [sum(sizes[: i + 1]) for i in range(len(sizes))]
    (
        out_bias_grad,
        first_gain_grad,
        first_shift_grad,
        down_bias_grad,
        second_gain_grad,
        second_shift_grad,
        query_bias_grad,
        value_bias_grad,
        up_bias_grad,
    ) = (packed[end - size : end] for end, size in zip(ends, sizes))
    return (
        layer_out,
        tokens_grad,
        qkv_shard.reshape(depth, 2, 3, unit).transpose(2, 0, 1, 3).reshape(3, depth, 2 * unit),
        query_bias_grad,
        value_bias_grad,
        out_shard.T,
        out_bias_grad,
        first_gain_grad,
        first_shift_grad,
        up_shard,
        up_bias_grad,
        down_shard.T,
        down_bias_grad,
        second_gain_grad,
        second_shift_grad,
    )


def solution(mesh):
    data_ways, split_ways = mesh.shape["dp"], mesh.shape["tensor"]
    fine = Mesh(mesh.devices.reshape(data_ways // 2, 2, split_ways), ALL)
    dp = ("chip", "core")
    in_specs = (
        P(ALL, None),
        P(ALL, None),
        P(ALL),
        P(ALL),
        P(dp, None, None),
        P(None, dp, "tensor"),
        P(),
        P(),
        P("tensor", dp),
        P(),
        P(),
        P(),
        P(dp, "tensor"),
        P(),
        P("tensor", dp),
        P(),
        P(),
        P(),
    )
    out_specs = (
        P(ALL, None),
        P(ALL, None),
        P(None, dp, "tensor"),
        P(),
        P(),
        P("tensor", dp),
        P(),
        P(),
        P(),
        P(dp, "tensor"),
        P(),
        P("tensor", dp),
        P(),
        P(),
        P(),
    )
    return jax.shard_map(
        on_device, mesh=fine, in_specs=in_specs, out_specs=out_specs, check_vma=False
    )
```
